32 devices in a mesh: groups: 2 (over x), stem: 8 (over z, y), cuts: 2 (over core).
Axes of the slice: x: 2, y: 2, z: 4, core: 2. Of those that a mesh axis runs over, the one named last changes fastest.
Arguments:
- stem: bfloat16 [4, 2, 4096, 1024], P(('groups', 'cuts'), None, 'stem'), parts along dimension 0, may hold values from -6 to 6
- edge_values: int32 [4, 4], P(('groups', 'cuts')), parts along dimension 0, may hold values from 0 to 1
- index_order: int32 [1024], replicated, may hold values from 0 to 1023, each once
- branch_first: bfloat16 [2, 1024, 1024], replicated, may hold values from -0.125 to 0.125
- branch_second: bfloat16 [2, 1024, 1024], replicated, may hold values from -0.125 to 0.125
- branch_third: bfloat16 [2, 1024, 256], replicated, may hold values from -0.125 to 0.125
- edge_table: float32 [16, 2, 256], replicated, may hold values from -6 to 6
- picks: int32 [4096], P('stem'), may hold values from 0 to 511, as said below
Outputs:
- amplitudes: float32 [2, 8192, 256], P(None, ('groups', 'stem')), parts along dimension 1
The draws below stay inside these ranges and needn't reach their ends.
There are 2 independent parts, one for each index of `groups`. The reference program is written for one: setup_inputs(seed, part) draws one part's arguments, and reference() takes and returns one part's arrays. A program takes and returns all parts, laid end to end along the dimension named above; an argument that names none is the same for every part. Nothing has to cross between parts.
Inputs may be any that keep to these rules, and one draw needn't show every extreme that they name: `index_order`: each number of 0 to 1023 once. `picks`: each aligned block of 512 entries names every number of 0 to 511 once.
All inputs are finite; a program needn't handle non-finite values.
Results may differ from the reference program's by a relative error of at most 0.0041.
Values may be sent and summed in bfloat16 or wider, within the bound.
No kernel may reach another device: no remote copies, remote signals or barrier semaphores. Data moves between devices by JAX's collectives and lax.ppermute only.
A program may use at most 64 MiB of HBM per device.

```python
import jax
import jax.numpy as jnp

K = 1024
KC = 256
ROWS_DEV = 512
PICKS = 512
EDGES = 4
CODES = 16
SLICES = 2
ROWS = 4096
OUT_ROWS = 4096
N_STEM = 8


def draw_picks(key, part):
    block_keys = jax.random.split(key, OUT_ROWS // ROWS_DEV)
    blocks = jax.vmap(lambda block_key: jax.random.permutation(block_key, ROWS_DEV))(block_keys)
    return blocks.reshape(-1).astype(jnp.int32)


def set_ends(drawn, rng, smallest, top_value):
    index_at = [jax.random.randint(jax.random.fold_in(rng, axis), (), 0, length) for axis, length in enumerate(drawn.shape)]
    longest = drawn.shape.index(max(drawn.shape))
    next_to = index_at[:longest] + [(index_at[longest] + 1) % drawn.shape[longest]] + index_at[longest + 1:]
    return drawn.at[tuple(index_at)].set(smallest).at[tuple(next_to)].set(top_value)


def level_of(key, shape, shards, low, high):
    def one(axis_at, shards_of):
        draws = jax.random.uniform(jax.random.fold_in(jax.random.fold_in(key, 6), axis_at), (shards_of,), jnp.float32, low / len(shards), high / len(shards))
        return jnp.repeat(jnp.exp(draws), shape[axis_at] // shards_of).reshape((-1,) + (1,) * (len(shape) - axis_at - 1))

    level = one(*shards[0])
    for cut in shards[1:]:
        level = level * one(*cut)
    return level


def scatter_about(own_key, extent, spread, limit, shards=(), held_as=jnp.bfloat16):
    array = jax.random.normal(own_key, extent, jnp.float32) * spread
    if len(shards) > 0:
        array = level_of(own_key, extent, shards, -0.22, 0.18) * array
    return jnp.clip(array, min=-limit, max=limit).astype(held_as)


def setup_inputs(seed: int = 0, part: int = 0) -> dict:
    splits = jax.random.split(jax.random.key(seed), 9)
    own_keys = jax.random.split(jax.random.fold_in(splits[8], part), 9)
    stem = scatter_about(own_keys[0], (SLICES, 2, ROWS, K), 1.0, 6.0, ((0, 2), (2, 8)))
    edge_values = set_ends(jax.random.randint(own_keys[1], (SLICES, EDGES), 0, 2), jax.random.fold_in(own_keys[1], 1), 0, 1).astype(jnp.int32)
    index_order = jax.random.permutation(splits[2], K).astype(jnp.int32)
    branch_first = scatter_about(splits[3], (2, K, K), (2 * K) ** -0.5, 0.125)
    branch_second = scatter_about(splits[4], (2, K, K), (2 * K) ** -0.5, 0.125)
    branch_third = scatter_about(splits[5], (2, K, KC), (2 * K) ** -0.5, 0.125)
    edge_table = scatter_about(splits[6], (CODES, 2, KC), 1.0, 6.0, (), jnp.float32)
    picks = draw_picks(jax.random.fold_in(splits[8], 71), part)
    return {"stem": stem, "edge_values": edge_values, "index_order": index_order, "branch_first": branch_first, "branch_second": branch_second, "branch_third": branch_third, "edge_table": edge_table, "picks": picks}


def complex_dot(operand, matrix):
    real = jnp.dot(operand[0], matrix[0], preferred_element_type=jnp.float32) - jnp.dot(operand[1], matrix[1], preferred_element_type=jnp.float32)
    imag = jnp.dot(operand[0], matrix[1], preferred_element_type=jnp.float32) + jnp.dot(operand[1], matrix[0], preferred_element_type=jnp.float32)
    return jnp.stack([real, imag])


def reference(stem, edge_values, index_order, branch_first, branch_second, branch_third, edge_table, picks):
    half_axis = N_STEM // 2
    block_rows = ROWS_DEV // N_STEM
    row_ids = (jnp.arange(N_STEM * PICKS, dtype=jnp.int32) // PICKS) * ROWS_DEV + picks
    powers = 2 ** jnp.arange(EDGES, dtype=jnp.int32)
    total = jnp.zeros((2, N_STEM * PICKS, KC), jnp.float32)
    for slice_id in range(SLICES):
        first = complex_dot(stem[slice_id], branch_first).astype(jnp.bfloat16)
        viewed = first.reshape(2, 2, half_axis, ROWS_DEV, 2, K // 2)
        swapped = jnp.transpose(viewed, (0, 4, 2, 3, 1, 5)).reshape(2, N_STEM * ROWS_DEV, K)
        permuted = jnp.take(swapped, index_order, axis=2)
        second = complex_dot(permuted, branch_second).astype(jnp.bfloat16)
        moved = jnp.swapaxes(second.reshape(2, N_STEM, N_STEM, block_rows, K), 1, 2).reshape(2, N_STEM * ROWS_DEV, K)
        picked = jnp.take(moved, row_ids, axis=1)
        third = complex_dot(picked, branch_third)
        code = jnp.sum(edge_values[slice_id] * powers)
        factor = edge_table[code]
        real = third[0] * factor[0][None, :] - third[1] * factor[1][None, :]
        imag = third[0] * factor[1][None, :] + third[1] * factor[0][None, :]
        total = total + jnp.stack([real, imag])
    return total
```

```python
import jax
import jax.numpy as jnp
from jax import lax
from jax.sharding import PartitionSpec as P


def dot32(left, right):
    return jnp.dot(left, right, preferred_element_type=jnp.float32)


def turned(matrix):
    half = matrix.shape[1] // 2
    return jnp.concatenate([-matrix[:, half:], matrix[:, :half]], axis=1)


def on_device(
    stem, edge_values, index_order, branch_first, branch_second, branch_third, edge_table, picks
):
    stem_size = lax.axis_size("stem")
    cut_size = lax.axis_size("cuts")
    half_size = stem_size // 2
    top_bit = lax.axis_index("stem") // half_size
    core = lax.axis_index("cuts")
    width = branch_first.shape[1]
    half_width = width // 2
    rows_dev = stem.shape[2]
    half_rows = rows_dev // 2
    block_rows = rows_dev // stem_size
    cols = branch_third.shape[2]
    swap = [(source, source ^ 1) for source in range(cut_size)]

    other_stem = lax.ppermute(stem, "cuts", swap)
    other_edges = lax.ppermute(edge_values, "cuts", swap)

    third_cat = jnp.concatenate([branch_third[0], branch_third[1]], axis=1)
    weight = dot32(branch_second[0], third_cat) + dot32(branch_second[1], turned(third_cat))
    powers = 2 ** jnp.arange(edge_values.shape[1], dtype=jnp.int32)

    def scaled(edges):
        code = jnp.sum(edges[0] * powers)
        factor = lax.dynamic_index_in_dim(edge_table, code, 0, keepdims=False)
        real, imag = weight[:, :cols], weight[:, cols:]
        return jnp.concatenate(
            [real * factor[0] - imag * factor[1], real * factor[1] + imag * factor[0]], axis=1
        ).astype(jnp.bfloat16)

    rows_of = lax.broadcasted_iota(jnp.int32, (half_width, width), 0) + top_bit * half_width
    chosen = (rows_of == index_order[None, :]).astype(jnp.bfloat16)
    first_half = lax.dynamic_slice_in_dim(branch_first, core * half_width, half_width, axis=2)

    total = None
    for one_stem, edges in ((stem, edge_values), (other_stem, other_edges)):
        ordered = dot32(chosen, scaled(edges)).astype(jnp.bfloat16)
        merged = (dot32(first_half[0], ordered) + dot32(first_half[1], turned(ordered))).astype(
            jnp.bfloat16
        )
        part = dot32(one_stem[0, 0], merged) + dot32(one_stem[0, 1], turned(merged))
        total = part if total is None else total + part
    sent = total.astype(jnp.bfloat16).reshape(stem_size, block_rows, 2 * cols)
    own = lax.all_to_all(sent, "stem", split_axis=0, concat_axis=0, tiled=True)
    own = own.reshape(rows_dev, 2 * cols)
    other = lax.ppermute(own, "cuts", swap)
    place = lax.broadcasted_iota(jnp.int32, (rows_dev, rows_dev), 1) % half_rows
    pick_own = (place + core * half_rows == picks[:, None]).astype(jnp.bfloat16)
    pick_other = (place + (1 - core) * half_rows == picks[:, None]).astype(jnp.bfloat16)
    rows = dot32(pick_own, own) + dot32(pick_other, other)
    return jnp.stack([rows[:, :cols], rows[:, cols:]])


def solution(mesh):
    return jax.shard_map(
        on_device,
        mesh=mesh,
        in_specs=(
            P(("groups", "cuts"), None, "stem", None),
            P(("groups", "cuts"), None),
            P(),
            P(),
            P(),
            P(),
            P(),
            P("stem"),
        ),
        out_specs=P(None, ("groups", "stem"), None),
        check_vma=False,
    )
```

```python
import jax
import jax.numpy as jnp
from jax import lax
from jax.experimental import pallas as pl
from jax.experimental.pallas import tpu as pltpu
from jax.sharding import PartitionSpec as P

VMEM_LIMIT = 60000 * 1024
SMEM = pl.BlockSpec(memory_space=pltpu.SMEM)
VMEM = pl.BlockSpec(memory_space=pltpu.VMEM)
ANY = pl.BlockSpec(memory_space=pl.ANY)
BF16 = jnp.bfloat16
F32 = jnp.float32


def dot32(left, right):
    return jnp.dot(left, right, preferred_element_type=F32)


def packed_product(real, imag, packed):
    half = packed.shape[1] // 2
    by_real = dot32(real, packed)
    by_imag = dot32(imag, packed)
    return jnp.concatenate(
        [by_real[:, :half] - by_imag[:, half:], by_real[:, half:] + by_imag[:, :half]], axis=1
    )


def first_product(stem_ref, first_ref):
    real = dot32(stem_ref[0], first_ref[0]) - dot32(stem_ref[1], first_ref[1])
    imag = dot32(stem_ref[0], first_ref[1]) + dot32(stem_ref[1], first_ref[0])
    return real.astype(BF16), imag.astype(BF16)


def edge_code(edges_ref):
    code = edges_ref[0, 0]
    for edge in range(1, edges_ref.shape[1]):
        code = code + edges_ref[0, edge] * (2**edge)
    return code


def scaled(value, edges_ref, table_ref):
    code = edge_code(edges_ref)
    factor = table_ref[code]
    half = value.shape[1] // 2
    real, imag = value[:, :half], value[:, half:]
    f_re, f_im = factor[0:1], factor[1:2]
    return jnp.concatenate([real * f_re - imag * f_im, real * f_im + imag * f_re], axis=1)


def rows_copy(stem_hbm, buffer, start, sem):
    rows = buffer.shape[1]
    return pltpu.make_async_copy(
        stem_hbm.at[0, :, pl.ds(pl.multiple_of(start, rows), rows), :], buffer, sem
    )


def half_copy(first_hbm, buffer, core, sem):
    width = buffer.shape[2]
    return pltpu.make_async_copy(
        first_hbm.at[:, :, pl.ds(pl.multiple_of(core * width, width), width)], buffer, sem
    )


def weight_body(
    where, edges, order, table, stem_hbm, first_hbm, second_hbm, third_hbm,
    weight_out, part_out,
    third_buf, packed, second_buf, stem_buf, first_buf, raw_weight, sems,
):
    top, core = where[0], where[1]
    cols = third_buf.shape[2]
    half_rows = stem_buf.shape[1]
    chunks, _, chunk_rows, _ = second_buf.shape
    copy_third = pltpu.make_async_copy(third_hbm, third_buf, sems.at[0])
    copy_third.start()
    copies = [
        pltpu.make_async_copy(
            second_hbm.at[:, pl.ds(chunk * chunk_rows, chunk_rows), :],
            second_buf.at[chunk],
            sems.at[3 + chunk],
        )
        for chunk in range(chunks)
    ]
    for copy in copies:
        copy.start()
    copy_stem = rows_copy(stem_hbm, stem_buf, (1 - top) * half_rows, sems.at[1])
    copy_stem.start()
    copy_first = half_copy(first_hbm, first_buf, core, sems.at[2])
    copy_first.start()
    copy_third.wait()
    packed[:, :cols] = third_buf[0]
    packed[:, cols:] = third_buf[1]
    for chunk, copy in enumerate(copies):
        copy.wait()
        raw_weight[pl.ds(chunk * chunk_rows, chunk_rows), :] = packed_product(
            second_buf[chunk, 0], second_buf[chunk, 1], packed[...]
        ).astype(BF16)
    half_width = weight_out.shape[0]
    row_ids = lax.broadcasted_iota(jnp.int32, (half_width, order.shape[1]), 0) + top * half_width
    chosen = (row_ids == order[...]).astype(F32).astype(BF16)
    weight_out[...] = dot32(chosen, raw_weight[...]).astype(BF16)
    copy_stem.wait()
    copy_first.wait()
    real, imag = first_product(stem_buf, first_buf)
    part_out[...] = scaled(packed_product(real, imag, weight_out[...]), edges, table)


def cross_body(
    where, edges, table, weight, part, stem_hbm, first_hbm,
    *rest,
):
    *outs, stem_buf, first_buf, sums, sems = rest
    top, core, spot = where[0], where[1], where[2]
    half_rows = stem_buf.shape[1]
    copy_stem = rows_copy(stem_hbm, stem_buf, (1 - top) * half_rows, sems.at[0])
    copy_stem.start()
    copy_first = half_copy(first_hbm, first_buf, core, sems.at[1])
    copy_first.start()
    copy_stem.wait()
    copy_first.wait()
    real, imag = first_product(stem_buf, first_buf)
    value = part[...] + scaled(packed_product(real, imag, weight[...]), edges, table)
    sums[...] = value.astype(BF16)
    block = outs[0].shape[0]
    for step, out in enumerate(outs):
        out[...] = sums[pl.ds(pl.multiple_of((spot ^ step) * block, block), block), :]


def near_body(
    where, edges, other_edges, table, weight, stem_hbm, other_hbm, first_hbm,
    *rest,
):
    *outs, stem_buf, other_buf, first_buf, sums, sems = rest
    top, core, spot = where[0], where[1], where[2]
    half_rows = stem_buf.shape[1]
    copy_stem = rows_copy(stem_hbm, stem_buf, top * half_rows, sems.at[0])
    copy_stem.start()
    copy_first = half_copy(first_hbm, first_buf, core, sems.at[1])
    copy_first.start()
    copy_other = rows_copy(other_hbm, other_buf, top * half_rows, sems.at[2])
    copy_other.start()
    copy_stem.wait()
    copy_first.wait()
    real, imag = first_product(stem_buf, first_buf)
    value = scaled(packed_product(real, imag, weight[...]), edges, table)
    copy_other.wait()
    real, imag = first_product(other_buf, first_buf)
    value = value + scaled(packed_product(real, imag, weight[...]), other_edges, table)
    sums[...] = value.astype(BF16)
    block = outs[0].shape[0]
    for step, out in enumerate(outs):
        out[...] = sums[pl.ds(pl.multiple_of((spot ^ step) * block, block), block), :]


def pick_body(where, picks, *rest):
    *blocks, out, gathered = rest
    top, core, spot = where[0], where[1], where[2]
    rows_dev = picks.shape[0]
    cols = out.shape[2]
    block = blocks[0].shape[0]
    count = len(blocks) // 2
    half_count = count // 2
    half_rows = rows_dev // 2
    for side in range(2):
        for step in range(count):
            at = (side * 2 + step // half_count) * half_rows
            slot = spot ^ (step % half_count)
            gathered[pl.ds(pl.multiple_of(at + slot * block, block), block), :] = blocks[
                side * count + step
            ][...]
    lane = lax.broadcasted_iota(jnp.int32, (rows_dev, half_rows), 1)
    wanted = picks[...]
    total = None
    for side in range(2):
        half = jnp.where(side == 0, core, 1 - core)
        chosen = (lane + half * half_rows == wanted).astype(F32).astype(BF16)
        for term in range(2):
            at = (side * 2 + term) * half_rows
            value = dot32(chosen, gathered[at : at + half_rows, :])
            total = value if total is None else total + value
    out[0] = total[:, :cols]
    out[1] = total[:, cols:]


def params():
    return pltpu.CompilerParams(vmem_limit_bytes=VMEM_LIMIT)


def on_device(
    stem, edge_values, index_order, branch_first, branch_second, branch_third, edge_table, picks
):
    stem_size = lax.axis_size("stem")
    cut_size = lax.axis_size("cuts")
    half_size = stem_size // 2
    width = branch_first.shape[1]
    half_width = width // 2
    rows_dev = stem.shape[2]
    half_rows = rows_dev // 2
    block_rows = rows_dev // stem_size
    cols = branch_third.shape[2]
    position = lax.axis_index("stem")
    core = lax.axis_index("cuts")
    where = jnp.stack([position // half_size, core, position % half_size]).astype(jnp.int32)
    swap = [(source, source ^ 1) for source in range(cut_size)]

    other_stem = lax.ppermute(stem, "cuts", swap)
    other_edges = lax.ppermute(edge_values, "cuts", swap)

    stem_buf = pltpu.VMEM((2, half_rows, width), BF16)
    first_buf = pltpu.VMEM((2, width, half_width), BF16)
    sums = pltpu.VMEM((half_rows, 2 * cols), BF16)
    chunks = 4
    weight, part = pl.pallas_call(
        weight_body,
        in_specs=[SMEM, SMEM, VMEM, VMEM, ANY, ANY, ANY, ANY],
        out_specs=[VMEM, VMEM],
        out_shape=[
            jax.ShapeDtypeStruct((half_width, 2 * cols), BF16),
            jax.ShapeDtypeStruct((half_rows, 2 * cols), F32),
        ],
        scratch_shapes=[
            pltpu.VMEM((2, width, cols), BF16),
            pltpu.VMEM((width, 2 * cols), BF16),
            pltpu.VMEM((chunks, 2, width // chunks, width), BF16),
            stem_buf,
            first_buf,
            pltpu.VMEM((width, 2 * cols), BF16),
            pltpu.SemaphoreType.DMA((3 + chunks,)),
        ],
        compiler_params=params(),
        name="weight",
    )(
        where, edge_values, index_order[None, :], edge_table, stem, branch_first, branch_second,
        branch_third,
    )

    block_shape = jax.ShapeDtypeStruct((block_rows, 2 * cols), BF16)
    far = pl.pallas_call(
        cross_body,
        in_specs=[SMEM, SMEM, VMEM, VMEM, VMEM, ANY, ANY],
        out_specs=[VMEM] * half_size,
        out_shape=[block_shape] * half_size,
        scratch_shapes=[stem_buf, first_buf, sums, pltpu.SemaphoreType.DMA((2,))],
        compiler_params=params(),
        name="cross",
    )(where, other_edges, edge_table, weight, part, other_stem, branch_first)

    def exchange(block, step):
        pairs = [(source, source ^ step) for source in range(stem_size)]
        return lax.ppermute(block, "stem", pairs)

    far = [exchange(block, half_size + step) for step, block in enumerate(far)]
    near = pl.pallas_call(
        near_body,
        in_specs=[SMEM, SMEM, SMEM, VMEM, VMEM, ANY, ANY, ANY],
        out_specs=[VMEM] * half_size,
        out_shape=[block_shape] * half_size,
        scratch_shapes=[stem_buf, stem_buf, first_buf, sums, pltpu.SemaphoreType.DMA((3,))],
        compiler_params=params(),
        name="near",
    )(where, edge_values, other_edges, edge_table, weight, stem, other_stem, branch_first)
    near = [near[0]] + [exchange(block, step) for step, block in enumerate(near) if step > 0]

    own = list(near) + list(far)
    other = [lax.ppermute(block, "cuts", swap) for block in own]
    return pl.pallas_call(
        pick_body,
        in_specs=[SMEM, VMEM] + [VMEM] * (2 * stem_size),
        out_specs=VMEM,
        out_shape=jax.ShapeDtypeStruct((2, rows_dev, cols), F32),
        scratch_shapes=[pltpu.VMEM((2 * rows_dev, 2 * cols), BF16)],
        compiler_params=params(),
        name="pick",
    )(where, picks[:, None], *own, *other)


def turned(matrix):
    half = matrix.shape[1] // 2
    return jnp.concatenate([-matrix[:, half:], matrix[:, :half]], axis=1)


def on_device_many(
    stem, edge_values, index_order, branch_first, branch_second, branch_third, edge_table, picks
):
    stem_size = lax.axis_size("stem")
    cut_size = lax.axis_size("cuts")
    half_size = stem_size // 2
    top_bit = lax.axis_index("stem") // half_size
    core = lax.axis_index("cuts")
    width = branch_first.shape[1]
    half_width = width // 2
    rows_dev = stem.shape[2]
    half_rows = rows_dev // 2
    block_rows = rows_dev // stem_size
    cols = branch_third.shape[2]
    swap = [(source, source ^ 1) for source in range(cut_size)]

    other_stem = lax.ppermute(stem, "cuts", swap)
    other_edges = lax.ppermute(edge_values, "cuts", swap)

    third_cat = jnp.concatenate([branch_third[0], branch_third[1]], axis=1)
    weight = dot32(branch_second[0], third_cat) + dot32(branch_second[1], turned(third_cat))
    powers = 2 ** jnp.arange(edge_values.shape[1], dtype=jnp.int32)

    def scaled(edges):
        code = jnp.sum(edges[0] * powers)
        factor = lax.dynamic_index_in_dim(edge_table, code, 0, keepdims=False)
        real, imag = weight[:, :cols], weight[:, cols:]
        return jnp.concatenate(
            [real * factor[0] - imag * factor[1], real * factor[1] + imag * factor[0]], axis=1
        ).astype(jnp.bfloat16)

    rows_of = lax.broadcasted_iota(jnp.int32, (half_width, width), 0) + top_bit * half_width
    chosen = (rows_of == index_order[None, :]).astype(jnp.bfloat16)
    first_half = lax.dynamic_slice_in_dim(branch_first, core * half_width, half_width, axis=2)

    total = None
    for one_stem, edges in ((stem, edge_values), (other_stem, other_edges)):
        ordered = dot32(chosen, scaled(edges)).astype(jnp.bfloat16)
        merged = (dot32(first_half[0], ordered) + dot32(first_half[1], turned(ordered))).astype(
            jnp.bfloat16
        )
        part = dot32(one_stem[0, 0], merged) + dot32(one_stem[0, 1], turned(merged))
        total = part if total is None else total + part
    sent = total.astype(jnp.bfloat16).reshape(stem_size, block_rows, 2 * cols)
    own = lax.all_to_all(sent, "stem", split_axis=0, concat_axis=0, tiled=True)
    own = own.reshape(rows_dev, 2 * cols)
    other = lax.ppermute(own, "cuts", swap)
    place = lax.broadcasted_iota(jnp.int32, (rows_dev, rows_dev), 1) % half_rows
    pick_own = (place + core * half_rows == picks[:, None]).astype(jnp.bfloat16)
    pick_other = (place + (1 - core) * half_rows == picks[:, None]).astype(jnp.bfloat16)
    rows = dot32(pick_own, own) + dot32(pick_other, other)
    return jnp.stack([rows[:, :cols], rows[:, cols:]])


def solution(mesh):
    return jax.shard_map(
        on_device if mesh.shape["stem"] <= 8 else on_device_many,
        mesh=mesh,
        in_specs=(
            P(("groups", "cuts"), None, "stem", None),
            P(("groups", "cuts"), None),
            P(),
            P(),
            P(),
            P(),
            P(),
            P("stem"),
        ),
        out_specs=P(None, ("groups", "stem"), None),
        check_vma=False,
    )
```

```python
import jax
import jax.numpy as jnp
from jax import lax
from jax.experimental import pallas as pl
from jax.experimental.pallas import tpu as pltpu
from jax.sharding import PartitionSpec as P

VMEM_LIMIT = 24 * 1024 * 1024
VMEM = pl.BlockSpec(memory_space=pltpu.VMEM)
ANY = pl.BlockSpec(memory_space=pl.ANY)
BF16 = jnp.bfloat16
F32 = jnp.float32
LANES = 128


def dot32(left, right):
    return jnp.dot(left, right, preferred_element_type=F32)


def packed_product(real, imag, packed):
    half = packed.shape[1] // 2
    by_real = dot32(real, packed)
    by_imag = dot32(imag, packed)
    return jnp.concatenate(
        [by_real[:, :half] - by_imag[:, half:], by_real[:, half:] + by_imag[:, :half]], axis=1
    )


def first_product(stem_ref, first_ref):
    real = dot32(stem_ref[0], first_ref[0]) - dot32(stem_ref[1], first_ref[1])
    imag = dot32(stem_ref[0], first_ref[1]) + dot32(stem_ref[1], first_ref[0])
    return real.astype(BF16), imag.astype(BF16)


def edge_factor(edges_ref, table_ref):
    edges = edges_ref[...]
    powers = jnp.left_shift(1, lax.broadcasted_iota(jnp.int32, edges.shape, 1))
    code = jnp.sum(edges * powers, axis=1, keepdims=True)
    factor = jnp.zeros(table_ref.shape[1:], F32)
    for entry in range(table_ref.shape[0]):
        factor = jnp.where(code == entry, table_ref[entry], factor)
    return factor


def scaled(value, factor):
    half = value.shape[1] // 2
    real, imag = value[:, :half], value[:, half:]
    f_re, f_im = factor[0:1], factor[1:2]
    return jnp.concatenate([real * f_re - imag * f_im, real * f_im + imag * f_re], axis=1)


def place():
    half_size = lax.axis_size("stem") // 2
    position = lax.axis_index("stem")
    return position // half_size, lax.axis_index("cuts"), position % half_size


def part_of(real_imag, weight, factor):
    return scaled(packed_product(real_imag[0], real_imag[1], weight[...]), factor)


def weight_body(
    edges_hbm, order_hbm, table_hbm, stem_hbm, first_hbm, second_hbm, third_hbm,
    weight_out, part_out, first_out, near_out, table_out, factor_out,
    third_buf, packed, second_buf, stem_buf, edges, order, raw_weight, sems,
):
    top, core, _ = place()
    cols = third_buf.shape[2]
    half_rows = stem_buf.shape[1]
    half_width = weight_out.shape[0]
    chunks, _, chunk_rows, _ = second_buf.shape

    def load(source, target, at):
        copy = pltpu.make_async_copy(source, target, sems.at[at])
        copy.start()
        return copy

    def stem_rows(start):
        return stem_hbm.at[0, :, pl.ds(pl.multiple_of(start, half_rows), half_rows), :]

    copy_third = load(third_hbm, third_buf, 0)
    copies = [
        load(second_hbm.at[:, pl.ds(chunk * chunk_rows, chunk_rows), :], second_buf.at[chunk], 8 + chunk)
        for chunk in range(chunks)
    ]
    copy_order = load(order_hbm, order, 1)
    copy_stem = load(stem_rows((1 - top) * half_rows), stem_buf, 2)
    copy_first = load(
        first_hbm.at[:, :, pl.ds(pl.multiple_of(core * half_width, half_width), half_width)], first_out, 3
    )
    copy_table = load(table_hbm, table_out, 4)
    copy_edges = load(edges_hbm, edges, 5)
    copy_near = load(stem_rows(top * half_rows), near_out, 6)

    copy_third.wait()
    packed[:, :cols] = third_buf[0]
    packed[:, cols:] = third_buf[1]
    for chunk, copy in enumerate(copies):
        copy.wait()
        raw_weight[pl.ds(chunk * chunk_rows, chunk_rows), :] = packed_product(
            second_buf[chunk, 0], second_buf[chunk, 1], packed[...]
        ).astype(BF16)
    copy_order.wait()
    row_ids = lax.broadcasted_iota(jnp.int32, (half_width, order.shape[1]), 0) + top * half_width
    chosen = (row_ids == order[...]).astype(F32).astype(BF16)
    weight_out[...] = dot32(chosen, raw_weight[...]).astype(BF16)
    copy_table.wait()
    copy_edges.wait()
    factor = edge_factor(edges, table_out)
    factor_out[...] = factor
    copy_stem.wait()
    copy_first.wait()
    part_out[...] = part_of(first_product(stem_buf, first_out), weight_out, factor)
    copy_near.wait()


def send_out(value, sums, outs, spot):
    sums[...] = value.astype(BF16)
    block = outs[0].shape[0]
    for step, out in enumerate(outs):
        out[...] = sums[pl.ds(pl.multiple_of((spot ^ step) * block, block), block), :]


def cross_body(edges, table, weight, part, stem, first, *rest):
    *outs, factor_out, sums = rest
    top, _, spot = place()
    half_rows = sums.shape[0]
    factor = edge_factor(edges, table)
    factor_out[...] = factor
    rows = stem.at[0, :, pl.ds(pl.multiple_of((1 - top) * half_rows, half_rows), half_rows), :]
    value = part[...] + part_of(first_product(rows, first), weight, factor)
    send_out(value, sums, outs, spot)


def near_body(factor, other_factor, weight, stem, other_stem, first, *rest):
    *outs, sums = rest
    top, _, spot = place()
    half_rows = sums.shape[0]
    rows = other_stem.at[0, :, pl.ds(pl.multiple_of(top * half_rows, half_rows), half_rows), :]
    value = part_of(first_product(stem, first), weight, factor[...])
    value = value + part_of(first_product(rows, first), weight, other_factor[...])
    send_out(value, sums, outs, spot)


def down_rows(row_ref):
    return jnp.concatenate(
        [
            jnp.transpose(jnp.broadcast_to(row_ref[:, start : start + LANES], (LANES, LANES)))
            for start in range(0, row_ref.shape[1], LANES)
        ],
        axis=0,
    )


def pick_body(picks, *rest):
    *blocks, out, gathered = rest
    _, core, spot = place()
    rows_dev = picks.shape[1]
    cols = out.shape[2]
    block = blocks[0].shape[0]
    count = len(blocks) // 2
    half_count = count // 2
    half_rows = rows_dev // 2
    for side in range(2):
        for step in range(count):
            at = (side * 2 + step // half_count) * half_rows
            slot = spot ^ (step % half_count)
            gathered[pl.ds(pl.multiple_of(at + slot * block, block), block), :] = blocks[
                side * count + step
            ][...]
    lane = lax.broadcasted_iota(jnp.int32, (rows_dev, LANES), 1)
    wanted = down_rows(picks)
    total = None
    for side in range(2):
        half = core if side == 0 else 1 - core
        chosen = jnp.concatenate(
            [
                (lane + (half * half_rows + start) == wanted).astype(F32).astype(BF16)
                for start in range(0, half_rows, LANES)
            ],
            axis=1,
        )
        for term in range(2):
            at = (side * 2 + term) * half_rows
            value = dot32(chosen, gathered[at : at + half_rows, :])
            total = value if total is None else total + value
    out[0] = total[:, :cols]
    out[1] = total[:, cols:]


def params():
    return pltpu.CompilerParams(vmem_limit_bytes=VMEM_LIMIT)


def pinned(*arrays, space=pltpu.VMEM):
    return [pltpu.with_memory_space_constraint(array, space) for array in arrays]


def on_device(
    stem, edge_values, index_order, branch_first, branch_second, branch_third, edge_table, picks
):
    stem_size = lax.axis_size("stem")
    half_size = stem_size // 2
    width = branch_first.shape[1]
    half_width = width // 2
    rows_dev = stem.shape[2]
    half_rows = rows_dev // 2
    block_rows = rows_dev // stem_size
    cols = branch_third.shape[2]
    swap = [(source, source ^ 1) for source in range(lax.axis_size("cuts"))]

    other_stem = lax.ppermute(stem, "cuts", swap)
    other_edges = lax.ppermute(edge_values, "cuts", swap)

    stem_half = pltpu.VMEM((2, half_rows, width), BF16)
    factor_like = pltpu.VMEM((2, cols), F32)
    sums = pltpu.VMEM((half_rows, 2 * cols), BF16)
    chunks = 4
    weight, part, first_half, near_stem, table, factor = pl.pallas_call(
        weight_body,
        in_specs=[ANY] * 7,
        out_specs=[VMEM] * 6,
        out_shape=[
            pltpu.VMEM((half_width, 2 * cols), BF16),
            pltpu.VMEM((half_rows, 2 * cols), F32),
            pltpu.VMEM((2, width, half_width), BF16),
            stem_half,
            pltpu.VMEM(edge_table.shape, F32),
            factor_like,
        ],
        scratch_shapes=[
            pltpu.VMEM((2, width, cols), BF16),
            pltpu.VMEM((width, 2 * cols), BF16),
            pltpu.VMEM((chunks, 2, width // chunks, width), BF16),
            stem_half,
            pltpu.VMEM(edge_values.shape, jnp.int32),
            pltpu.VMEM((1, width), jnp.int32),
            pltpu.VMEM((width, 2 * cols), BF16),
            pltpu.SemaphoreType.DMA((8 + chunks,)),
        ],
        compiler_params=params(),
        name="weight",
    )(
        *pinned(
            edge_values, index_order[None, :], edge_table, stem, branch_first, branch_second,
            branch_third, space=pltpu.HBM,
        )
    )

    block_like = pltpu.VMEM((block_rows, 2 * cols), BF16)
    other_edges, other_stem = pinned(other_edges, other_stem)
    *far, other_factor = pl.pallas_call(
        cross_body,
        in_specs=[VMEM] * 6,
        out_specs=[VMEM] * (half_size + 1),
        out_shape=[block_like] * half_size + [factor_like],
        scratch_shapes=[sums],
        compiler_params=params(),
        name="cross",
    )(other_edges, *pinned(table, weight, part), other_stem, *pinned(first_half))

    def exchange(block, step):
        pairs = [(source, source ^ step) for source in range(stem_size)]
        return lax.ppermute(block, "stem", pairs)

    far = [exchange(block, half_size + step) for step, block in enumerate(far)]
    near = pl.pallas_call(
        near_body,
        in_specs=[VMEM] * 6,
        out_specs=[VMEM] * half_size,
        out_shape=[block_like] * half_size,
        scratch_shapes=[sums],
        compiler_params=params(),
        name="near",
    )(*pinned(factor, other_factor, weight, near_stem), other_stem, *pinned(first_half))
    near = [near[0]] + [exchange(block, step) for step, block in enumerate(near) if step > 0]
    own = near + far
    other = [lax.ppermute(block, "cuts", swap) for block in own]
    return pl.pallas_call(
        pick_body,
        in_specs=[VMEM] * (1 + 2 * stem_size),
        out_specs=VMEM,
        out_shape=jax.ShapeDtypeStruct((2, rows_dev, cols), F32),
        scratch_shapes=[pltpu.VMEM((2 * rows_dev, 2 * cols), BF16)],
        compiler_params=params(),
        name="pick",
    )(picks[None, :], *pinned(*own, *other))


def turned(matrix):
    half = matrix.shape[1] // 2
    return jnp.concatenate([-matrix[:, half:], matrix[:, :half]], axis=1)


def on_device_many(
    stem, edge_values, index_order, branch_first, branch_second, branch_third, edge_table, picks
):
    stem_size = lax.axis_size("stem")
    cut_size = lax.axis_size("cuts")
    half_size = stem_size // 2
    top_bit = lax.axis_index("stem") // half_size
    core = lax.axis_index("cuts")
    width = branch_first.shape[1]
    half_width = width // 2
    rows_dev = stem.shape[2]
    half_rows = rows_dev // 2
    block_rows = rows_dev // stem_size
    cols = branch_third.shape[2]
    swap = [(source, source ^ 1) for source in range(cut_size)]

    other_stem = lax.ppermute(stem, "cuts", swap)
    other_edges = lax.ppermute(edge_values, "cuts", swap)

    third_cat = jnp.concatenate([branch_third[0], branch_third[1]], axis=1)
    weight = dot32(branch_second[0], third_cat) + dot32(branch_second[1], turned(third_cat))
    powers = 2 ** jnp.arange(edge_values.shape[1], dtype=jnp.int32)

    def scaled(edges):
        code = jnp.sum(edges[0] * powers)
        factor = lax.dynamic_index_in_dim(edge_table, code, 0, keepdims=False)
        real, imag = weight[:, :cols], weight[:, cols:]
        return jnp.concatenate(
            [real * factor[0] - imag * factor[1], real * factor[1] + imag * factor[0]], axis=1
        ).astype(jnp.bfloat16)

    rows_of = lax.broadcasted_iota(jnp.int32, (half_width, width), 0) + top_bit * half_width
    chosen = (rows_of == index_order[None, :]).astype(jnp.bfloat16)
    first_half = lax.dynamic_slice_in_dim(branch_first, core * half_width, half_width, axis=2)

    total = None
    for one_stem, edges in ((stem, edge_values), (other_stem, other_edges)):
        ordered = dot32(chosen, scaled(edges)).astype(jnp.bfloat16)
        merged = (dot32(first_half[0], ordered) + dot32(first_half[1], turned(ordered))).astype(
            jnp.bfloat16
        )
        part = dot32(one_stem[0, 0], merged) + dot32(one_stem[0, 1], turned(merged))
        total = part if total is None else total + part
    sent = total.astype(jnp.bfloat16).reshape(stem_size, block_rows, 2 * cols)
    own = lax.all_to_all(sent, "stem", split_axis=0, concat_axis=0, tiled=True)
    own = own.reshape(rows_dev, 2 * cols)
    other = lax.ppermute(own, "cuts", swap)
    place = lax.broadcasted_iota(jnp.int32, (rows_dev, rows_dev), 1) % half_rows
    pick_own = (place + core * half_rows == picks[:, None]).astype(jnp.bfloat16)
    pick_other = (place + (1 - core) * half_rows == picks[:, None]).astype(jnp.bfloat16)
    rows = dot32(pick_own, own) + dot32(pick_other, other)
    return jnp.stack([rows[:, :cols], rows[:, cols:]])


def solution(mesh):
    return jax.shard_map(
        on_device if mesh.shape["stem"] <= 8 else on_device_many,
        mesh=mesh,
        in_specs=(
            P(("groups", "cuts"), None, "stem", None),
            P(("groups", "cuts"), None),
            P(),
            P(),
            P(),
            P(),
            P(),
            P("stem"),
        ),
        out_specs=P(None, ("groups", "stem"), None),
        check_vma=False,
    )
```
